32 devices in a mesh: grp: 2 (over x), lat: 8 (over z, y), lon: 2 (over core).
Axes of the slice: x: 2, y: 2, z: 4, core: 2. Of those that a mesh axis runs over, the one named last changes fastest.
Arguments:
- fields: bfloat16 [4, 128, 384, 256], P('grp', 'lat', 'lon'), parts along dimension 0
- mix_gain: float32 [2, 256], replicated, may hold values from 0.1 to 1.9
- lat_weight: bfloat16 [2, 5, 2, 128, 128], replicated, may hold values from -0.25 to 0.25
- lon_weight: bfloat16 [2, 5, 2, 128, 128], replicated, may hold values from -0.25 to 0.25
- mlp_gain: float32 [256], replicated, may hold values from 0.1 to 1.9
- w_in: bfloat16 [256, 1024], replicated, may hold values from -0.375 to 0.375
- w_out: bfloat16 [1024, 256], replicated, may hold values from -0.1875 to 0.1875
- lat_dilation: int32 [2], replicated, may hold values from 1 to 4, as said below
- lon_dilation: int32 [2], replicated, may hold values from 1 to 24, as said below
- ocean: int32 [256, 384], P(('grp', 'lat'), 'lon'), parts along dimension 0, may hold values 0 or 1
Outputs:
- mixed: bfloat16 [4, 128, 384, 256], P('grp', 'lat', 'lon'), parts along dimension 0
The draws below stay inside these ranges and needn't reach their ends.
There are 2 independent parts, one for each index of `grp`. The reference program is written for one: setup_inputs(seed, part) draws one part's arguments, and reference() takes and returns one part's arrays. A program takes and returns all parts, laid end to end along the dimension named above; an argument that names none is the same for every part. Nothing has to cross between parts.
Inputs may be any that keep to these rules, and one draw needn't show every extreme that they name: `lat_dilation`: 4 is taken by exactly one layer in every draw. `lon_dilation`: 24 is taken by exactly one layer in every draw.
All inputs are finite; a program needn't handle non-finite values. No bound on the sum of `ocean` on one device may be relied on, other than what follows from the above.
Results may differ from the reference program's by a relative error of at most 0.0075.
Values may be sent and summed in bfloat16 or wider, within the bound.
A program may use at most 128 MiB of HBM per device.

```python
import math
import jax
import jax.numpy as jnp
from jax import lax

C = 256
F = 1024
GROUPS = 2
CG = 128
TAPS = 5
LAYERS = 2
B = 2
MAXDIL_LAT = 4
MAXDIL_LON = 24
LAT = 128
LON = 384


def draw_fields(key, part):
    shape = (B, LAT, LON, C)
    first, second, third = jax.random.split(key, 3)
    base = jnp.clip(jax.random.normal(first, shape, jnp.float32), -6.0, 6.0)
    cell_scale = jnp.exp(jax.random.uniform(second, (B, LAT, LON, 1), jnp.float32, -0.5 * math.log(10.0), 0.5 * math.log(10.0)))
    chan_scale = jnp.exp(jax.random.uniform(third, (C,), jnp.float32, -0.5 * math.log(10.0), 0.5 * math.log(10.0)))
    return (base * cell_scale * chan_scale * 0.5).astype(jnp.bfloat16)


def dilation_draw(key, largest):
    values = jax.random.randint(key, (LAYERS,), 1, largest)
    chosen = jax.random.randint(jax.random.fold_in(key, 7), (), 0, LAYERS)
    return jnp.where(jnp.arange(LAYERS) == chosen, largest, values).astype(jnp.int32)


def draw_lat_dilation(key, part):
    return dilation_draw(jax.random.fold_in(key, 11), MAXDIL_LAT)


def draw_lon_dilation(key, part):
    return dilation_draw(jax.random.fold_in(key, 13), MAXDIL_LON)


def with_ends(drawn, key, smallest, high):
    dims = drawn.shape
    spot = [jax.random.randint(jax.random.fold_in(key, axis), (), 0, dims[axis]) for axis in range(len(dims))]
    drawn = drawn.at[tuple(spot)].set(smallest)
    longest = dims.index(max(dims))
    spot[longest] = (spot[longest] + 1) % dims[longest]
    return drawn.at[tuple(spot)].set(high)


def normal_values(key, extent, deviation, reach, held_as=jnp.bfloat16):
    return jnp.clip(deviation * jax.random.normal(key, extent, jnp.float32), -reach, reach).astype(held_as)


def setup_inputs(seed: int = 0, part: int = 0) -> dict:
    seeds = jax.random.split(jax.random.key(seed), 11)
    part_splits = jax.random.split(jax.random.fold_in(seeds[10], part), 11)
    return {
        "fields": draw_fields(jax.random.fold_in(jax.random.fold_in(seeds[10], part), 71), part),
        "mix_gain": jnp.clip(1.0 + 0.18 * jax.random.normal(seeds[1], (LAYERS, C), jnp.float32), 0.1, 1.9),
        "lat_weight": normal_values(seeds[2], (LAYERS, TAPS, GROUPS, CG, CG), (TAPS * CG) ** -0.5, 0.25),
        "lon_weight": normal_values(seeds[3], (LAYERS, TAPS, GROUPS, CG, CG), (TAPS * CG) ** -0.5, 0.25),
        "mlp_gain": jnp.clip(1.0 + 0.18 * jax.random.normal(seeds[4], (C,), jnp.float32), 0.1, 1.9),
        "w_in": normal_values(seeds[5], (C, F), C ** -0.5, 0.375),
        "w_out": normal_values(seeds[6], (F, C), F ** -0.5, 0.1875),
        "lat_dilation": draw_lat_dilation(jax.random.fold_in(seeds[10], 71), part),
        "lon_dilation": draw_lon_dilation(jax.random.fold_in(seeds[10], 71), part),
        "ocean": with_ends((jax.random.randint(part_splits[9], (LAT, LON), 0, 3) < 2).astype(jnp.int32), jax.random.fold_in(part_splits[9], 1), 0, 1),
    }


def rms_scale(state, gain):
    wide = state.astype(jnp.float32)
    power = lax.optimization_barrier(jnp.mean(wide * wide, axis=-1, keepdims=True))
    return wide * lax.rsqrt(power + 1e-06) * gain

def grouped(piece, weight):
    shape = piece.shape
    split = piece.reshape(shape[:-1] + (GROUPS, CG)).astype(jnp.float32)
    result = jnp.einsum('blwgc,gcd->blwgd', split, weight.astype(jnp.float32))
    return result.reshape(shape)

def reference(fields, mix_gain, lat_weight, lon_weight, mlp_gain, w_in, w_out, lat_dilation, lon_dilation, ocean):
    half = TAPS // 2
    lat_reach = half * MAXDIL_LAT
    lon_reach = half * MAXDIL_LON
    wet = ocean.astype(jnp.float32)[None, :, :, None]
    state = fields
    for layer in range(LAYERS):
        normed = rms_scale(state, mix_gain[layer]).astype(jnp.bfloat16)
        padded = jnp.pad(normed, ((0, 0), (lat_reach, lat_reach), (0, 0), (0, 0)))
        total = jnp.zeros(normed.shape, jnp.float32)
        for tap in range(TAPS):
            start = (lat_reach + (tap - half) * lat_dilation[layer]).astype(jnp.int32)
            piece = lax.dynamic_slice_in_dim(padded, start, LAT, 1)
            total = total + grouped(piece, lat_weight[layer, tap])
        across = total.astype(jnp.bfloat16)
        wrapped = jnp.concatenate([across[:, :, LON - lon_reach:], across, across[:, :, :lon_reach]], 2)
        total = jnp.zeros(normed.shape, jnp.float32)
        for tap in range(TAPS):
            start = (lon_reach + (tap - half) * lon_dilation[layer]).astype(jnp.int32)
            piece = lax.dynamic_slice_in_dim(wrapped, start, LON, 2)
            total = total + grouped(piece, lon_weight[layer, tap])
        state = (state.astype(jnp.float32) + wet * total).astype(jnp.bfloat16)
    lifted = rms_scale(state, mlp_gain).astype(jnp.bfloat16).reshape(-1, C)
    hidden = jax.nn.silu(jnp.dot(lifted, w_in, preferred_element_type=jnp.float32)).astype(jnp.bfloat16)
    update = jnp.dot(hidden, w_out, preferred_element_type=jnp.float32).reshape(state.shape)
    return (state.astype(jnp.float32) + update).astype(jnp.bfloat16)
```

```python
import functools

import jax
import jax.numpy as jnp
from jax import lax
from jax.experimental import pallas as pl
from jax.experimental.pallas import tpu as pltpu
from jax.sharding import PartitionSpec as P

C = 256
GROUPS = 2
CG = 128
TAPS = 5
HALF = 2
LAYERS = 2
MAXDIL_LAT = 4
MAXDIL_LON = 24
REACH = HALF * MAXDIL_LAT
LON_REACH = HALF * MAXDIL_LON
TILE_COLS = 32
TILE_ROWS = 4
VMEM_LIMIT = 48 * 1024 * 1024
CHUNKS = ((0, 96), (96, 96))


def scaled(wide, gain):
    power = jnp.mean(wide * wide, axis=-1, keepdims=True)
    return wide * lax.rsqrt(power + 1e-06) * gain


def block_diagonal(weight):
    zero = jnp.zeros_like(weight[:, :, 0])
    top = jnp.concatenate([weight[:, :, 0], zero], -1)
    low = jnp.concatenate([zero, weight[:, :, 1]], -1)
    return jnp.concatenate([top, low], -2).reshape(LAYERS, TAPS * C, C)


def conv_rows(held, weight_ref, dilation, first, count):
    pieces = []
    for tap in range(TAPS):
        piece = held[pl.ds(first + (tap - HALF) * dilation, count)]
        pieces.append(piece.reshape(count * held.shape[1], C))
    total = jnp.dot(
        jnp.concatenate(pieces, 1), weight_ref[...], preferred_element_type=jnp.float32
    )
    return total.astype(jnp.bfloat16).reshape(count, held.shape[1], C)


def lat_first(info, own, came, north, south, gain, weight, across, state, held):
    member, dilation = info[0], info[1]
    rows = came.shape[0]
    held[0:REACH] = scaled(north[...].astype(jnp.float32), gain[...]).astype(jnp.bfloat16)
    held[pl.ds(REACH + 2 * rows, REACH)] = scaled(
        south[...].astype(jnp.float32), gain[...]
    ).astype(jnp.bfloat16)
    for ref, place in ((own.at[0], member), (came, 1 - member)):
        value = ref[...]
        state[pl.ds(place * rows, rows)] = value
        held[pl.ds(REACH + place * rows, rows)] = scaled(
            value.astype(jnp.float32), gain[...]
        ).astype(jnp.bfloat16)
    for part in range(2):
        across[part * rows : (part + 1) * rows] = conv_rows(
            held, weight, dilation, REACH + part * rows, rows
        )


def lat_inner(info, edge, inner, weight, across, held):
    half = edge.shape[0] // 2
    rows = inner.shape[0]
    held[0:half] = edge[0:half]
    held[half : half + rows] = inner[...]
    held[half + rows : half + rows + half] = edge[half:]
    across[...] = conv_rows(held, weight, info[1], half, rows)


def lat_edge(info, edge, inner, north, south, weight, across, held):
    half = edge.shape[0] // 2
    rows = inner.shape[0]
    held[0:REACH] = north[...]
    held[REACH : REACH + half] = edge[0:half]
    held[REACH + half : REACH + half + rows] = inner[...]
    held[REACH + half + rows : REACH + 2 * half + rows] = edge[half:]
    held[REACH + 2 * half + rows : 2 * REACH + 2 * half + rows] = south[...]
    across[0:half] = conv_rows(held, weight, info[1], REACH, half)
    across[half:] = conv_rows(held, weight, info[1], REACH + half + rows, half)


def lon_total(info, pieces, weight, wide):
    at = 0
    for piece in pieces:
        width = piece.shape[1]
        for group in range(GROUPS):
            wide[group, :, at : at + width] = piece[
                :, :, group * CG : (group + 1) * CG
            ].astype(jnp.float32)
        at += width
    cols = at - 2 * LON_REACH
    taps = []
    for tap in range(TAPS):
        start = LON_REACH + (tap - HALF) * info[2]
        for group in range(GROUPS):
            piece = wide[group, :, pl.ds(start, cols), :]
            taps.append(piece.astype(jnp.bfloat16).reshape(TILE_ROWS * cols, CG))
    return jnp.dot(
        jnp.concatenate(taps, 1), weight[...], preferred_element_type=jnp.float32
    )


def wet_column(ocean):
    return jnp.concatenate([ocean[0][:, r : r + 1] for r in range(TILE_ROWS)], 0)


def lon_first(count, info, *refs):
    pieces, states = refs[: count + 2], refs[count + 2 : 2 * count + 2]
    ocean, gain, weight, state_out, normed_out, wide = refs[2 * count + 2 :]
    total = lon_total(info, pieces, weight, wide)
    total = (total * wet_column(ocean)).reshape(state_out.shape)
    at = 0
    for ref in states:
        width = ref.shape[1]
        new = ref[...].astype(jnp.float32) + total[:, at : at + width]
        new = new.astype(jnp.bfloat16)
        state_out[:, at : at + width] = new
        normed_out[:, at : at + width] = scaled(new.astype(jnp.float32), gain[...]).astype(
            jnp.bfloat16
        )
        at += width


def lon_mlp(info, left, middle, right, state, ocean, gain, weight, w_in, w_out, out, wide):
    total = lon_total(info, (left, middle, right), weight, wide)
    size = total.shape[0]
    old = state[...].astype(jnp.float32).reshape(size, C)
    new = (old + total * wet_column(ocean)).astype(jnp.bfloat16).astype(jnp.float32)
    lifted = scaled(new, gain[...]).astype(jnp.bfloat16)
    value = jnp.dot(lifted, w_in[...], preferred_element_type=jnp.float32)
    hidden = (value / (1.0 + jnp.exp(-value))).astype(jnp.bfloat16)
    update = jnp.dot(hidden, w_out[...], preferred_element_type=jnp.float32)
    out[...] = (new + update).astype(jnp.bfloat16).reshape(out.shape)


def whole(array):
    dims = array.ndim
    return pl.BlockSpec(array.shape, lambda *_: (0,) * dims, pipeline_mode=pl.Buffered(1))


def launch(body, info, grid, specs, out_specs, out_shape, scratch, flops, args):
    moved = sum(a.size * a.dtype.itemsize for a in args[1:])
    return pl.pallas_call(
        body,
        grid_spec=pltpu.PrefetchScalarGridSpec(
            num_scalar_prefetch=1,
            grid=(grid,),
            in_specs=specs,
            out_specs=out_specs,
            scratch_shapes=scratch,
        ),
        out_shape=out_shape,
        compiler_params=pltpu.CompilerParams(vmem_limit_bytes=VMEM_LIMIT),
        cost_estimate=pl.CostEstimate(flops=flops, bytes_accessed=moved, transcendentals=0),
    )(info, *args)


def on_device(
    fields,
    mix_gain,
    lat_weight,
    lon_weight,
    mlp_gain,
    w_in,
    w_out,
    lat_dilation,
    lon_dilation,
    ocean,
):
    bf16 = jnp.bfloat16
    rows, cols = fields.shape[1:3]
    count = lax.axis_size("lat")
    around = lax.axis_size("lon")
    member = lax.rem(lax.axis_index("lat"), 2).astype(jnp.int32)
    swap_pairs = [(i, i ^ 1) for i in range(count)]
    south_pairs = [(i, i + 2) for i in range(count - 2)]
    north_pairs = [(i + 2, i) for i in range(count - 2)]
    east_pairs = [(i, (i + 1) % around) for i in range(around)]
    west_pairs = [((i + 1) % around, i) for i in range(around)]

    def swap(x):
        return lax.ppermute(x, "lat", swap_pairs)

    def lat_halo(top, bottom):
        return lax.ppermute(bottom, "lat", south_pairs), lax.ppermute(top, "lat", north_pairs)

    def lon_halo(head, tail):
        return lax.ppermute(tail, "lon", east_pairs), lax.ppermute(head, "lon", west_pairs)

    infos = [
        jnp.stack([member, lat_dilation[l], lon_dilation[l], jnp.int32(0)]) for l in range(LAYERS)
    ]
    lat_w = block_diagonal(lat_weight)
    lon_w = block_diagonal(lon_weight)

    def lat_flops(r, c):
        return 2 * r * c * TAPS * C * C

    other = lax.dynamic_index_in_dim(fields, 1 - member, 0, False)
    came = [swap(other[:, a : a + n]) for a, n in CHUNKS]
    own = lax.dynamic_index_in_dim(fields, member, 0, False)
    across, state = [], []
    for (a, n), got in zip(CHUNKS, came):
        mine = own[:, a : a + n]
        top = jnp.where(member == 0, mine[:REACH], got[:REACH])
        bottom = jnp.where(member == 0, got[rows - REACH :], mine[rows - REACH :])
        north, south = lat_halo(top, bottom)
        base = a // TILE_COLS
        strip = lambda size: pl.BlockSpec((size, TILE_COLS, C), lambda i, s: (0, i, 0))
        gain = mix_gain[0:1]
        shape = jax.ShapeDtypeStruct((2 * rows, n, C), bf16)
        got_across, got_state = launch(
            lat_first,
            infos[0],
            n // TILE_COLS,
            [
                pl.BlockSpec(
                    (1, rows, TILE_COLS, C), lambda i, s, base=base: (s[0], 0, base + i, 0)
                ),
                strip(rows),
                strip(REACH),
                strip(REACH),
                whole(gain),
                whole(lat_w[0]),
            ],
            [strip(2 * rows)] * 2,
            [shape] * 2,
            [pltpu.VMEM((2 * rows + 2 * REACH, TILE_COLS, C), bf16)],
            lat_flops(2 * rows, n),
            (fields, got, north, south, gain, lat_w[0]),
        )
        across.append(got_across)
        state.append(got_state)

    wet = ocean.astype(jnp.float32)
    wet_came = swap(wet)
    wet = jnp.where(
        member == 0, jnp.concatenate([wet, wet_came], 0), jnp.concatenate([wet_came, wet], 0)
    )
    tiles = 2 * rows // TILE_ROWS
    wet = wet.reshape(tiles, TILE_ROWS, cols).transpose(0, 2, 1)
    edge_tiles = REACH // TILE_ROWS
    inner_tiles = tiles - 2 * edge_tiles
    wet_edge = jnp.concatenate([wet[:edge_tiles], wet[tiles - edge_tiles :]], 0)
    wet_inner = wet[edge_tiles : tiles - edge_tiles]

    left, right = lon_halo(across[0][:, :LON_REACH], across[-1][:, -LON_REACH:])
    wide = pltpu.VMEM((GROUPS, TILE_ROWS, cols + 2 * LON_REACH, CG), jnp.float32)

    def first_pair(wets, to_tile):
        gain = mix_gain[1:2]
        band = lambda width: pl.BlockSpec(
            (TILE_ROWS, width, C), lambda i, s: (to_tile(i), 0, 0)
        )
        widths = [n for _, n in CHUNKS]
        count_tiles = wets.shape[0]
        shape = jax.ShapeDtypeStruct((count_tiles * TILE_ROWS, cols, C), bf16)
        return launch(
            functools.partial(lon_first, len(CHUNKS)),
            infos[0],
            count_tiles,
            [band(LON_REACH)]
            + [band(n) for n in widths]
            + [band(LON_REACH)]
            + [band(n) for n in widths]
            + [
                pl.BlockSpec((1, cols, TILE_ROWS), lambda i, s: (i, 0, 0)),
                whole(gain),
                whole(lon_w[0]),
            ],
            [pl.BlockSpec((TILE_ROWS, cols, C), lambda i, s: (i, 0, 0))] * 2,
            [shape] * 2,
            [wide],
            lat_flops(count_tiles * TILE_ROWS, cols),
            (left, *across, right, *state, wets, gain, lon_w[0]),
        )

    edge_state, edge_normed = first_pair(
        wet_edge, lambda i: jnp.where(i < edge_tiles, i, i + inner_tiles)
    )
    north, south = lat_halo(edge_normed[:REACH], edge_normed[REACH:])
    inner_state, inner_normed = first_pair(wet_inner, lambda i: i + edge_tiles)

    inner_rows = inner_state.shape[0]
    strip = lambda size: pl.BlockSpec((size, TILE_COLS, C), lambda i, s: (0, i, 0))
    inner_across = launch(
        lat_inner,
        infos[1],
        cols // TILE_COLS,
        [strip(2 * REACH), strip(inner_rows), whole(lat_w[1])],
        strip(inner_rows),
        jax.ShapeDtypeStruct((inner_rows, cols, C), bf16),
        [pltpu.VMEM((2 * REACH + inner_rows, TILE_COLS, C), bf16)],
        lat_flops(inner_rows, cols),
        (edge_normed, inner_normed, lat_w[1]),
    )
    edge_across = launch(
        lat_edge,
        infos[1],
        cols // TILE_COLS,
        [strip(2 * REACH), strip(inner_rows), strip(REACH), strip(REACH), whole(lat_w[1])],
        strip(2 * REACH),
        jax.ShapeDtypeStruct((2 * REACH, cols, C), bf16),
        [pltpu.VMEM((4 * REACH + inner_rows, TILE_COLS, C), bf16)],
        lat_flops(2 * REACH, cols),
        (edge_normed, inner_normed, north, south, lat_w[1]),
    )

    gain = mlp_gain[None]

    def second(acr, halo, old, wets, base, number):
        info = infos[1].at[3].set(base)
        band = lambda width: pl.BlockSpec(
            (TILE_ROWS, width, C), lambda i, s: (s[3] + i, 0, 0)
        )
        size = number * TILE_ROWS
        return launch(
            lon_mlp,
            info,
            number,
            [
                band(LON_REACH),
                band(cols),
                band(LON_REACH),
                band(cols),
                pl.BlockSpec((1, cols, TILE_ROWS), lambda i, s: (s[3] + i, 0, 0)),
                whole(gain),
                whole(lon_w[1]),
                whole(w_in),
                whole(w_out),
            ],
            pl.BlockSpec((TILE_ROWS, cols, C), lambda i, s: (i, 0, 0)),
            jax.ShapeDtypeStruct((size, cols, C), bf16),
            [wide],
            lat_flops(size, cols) + 16 * size * cols * C * C,
            (halo[0], acr, halo[1], old, wets, gain, lon_w[1], w_in, w_out),
        )

    inner_halo = lon_halo(inner_across[:, :LON_REACH], inner_across[:, -LON_REACH:])
    edge_halo = lon_halo(edge_across[:, :LON_REACH], edge_across[:, -LON_REACH:])
    inner_half = inner_tiles // 2
    send_inner = second(
        inner_across, inner_halo, inner_state, wet_inner, (1 - member) * inner_half, inner_half
    )
    back_inner = swap(send_inner)
    keep_inner = second(
        inner_across, inner_halo, inner_state, wet_inner, member * inner_half, inner_half
    )
    send_edge = second(
        edge_across, edge_halo, edge_state, wet_edge, (1 - member) * edge_tiles, edge_tiles
    )
    back_edge = swap(send_edge)
    keep_edge = second(
        edge_across, edge_halo, edge_state, wet_edge, member * edge_tiles, edge_tiles
    )
    out = jnp.zeros(fields.shape, bf16)
    edge_at = member * (rows - REACH)
    inner_at = (1 - member) * REACH
    for piece, sample, at in (
        (keep_inner, member, inner_at),
        (keep_edge, member, edge_at),
        (back_inner, 1 - member, inner_at),
        (back_edge, 1 - member, edge_at),
    ):
        out = lax.dynamic_update_slice(out, piece[None], (sample, at, 0, 0))
    return out


def solution(mesh):
    return jax.shard_map(
        on_device,
        mesh=mesh,
        in_specs=(
            P("grp", "lat", "lon", None),
            P(),
            P(),
            P(),
            P(),
            P(),
            P(),
            P(),
            P(),
            P(("grp", "lat"), "lon"),
        ),
        out_specs=P("grp", "lat", "lon", None),
        check_vma=False,
    )
```

```python
import functools

import jax
import jax.numpy as jnp
from jax import lax
from jax.experimental import pallas as pl
from jax.experimental.pallas import tpu as pltpu
from jax.sharding import PartitionSpec as P

C = 256
GROUPS = 2
CG = 128
TAPS = 5
HALF = 2
LAYERS = 2
MAXDIL_LAT = 4
MAXDIL_LON = 24
REACH = HALF * MAXDIL_LAT
LON_REACH = HALF * MAXDIL_LON
TILE_COLS = LON_REACH
TILE_ROWS = 4
VMEM_LIMIT = 48 * 1024 * 1024


def scaled(wide, gain):
    power = jnp.mean(wide * wide, axis=-1, keepdims=True)
    return wide * lax.rsqrt(power + 1e-06) * gain


def block_diagonal(weight):
    zero = jnp.zeros_like(weight[:, 0])
    top = jnp.concatenate([weight[:, 0], zero], -1)
    low = jnp.concatenate([zero, weight[:, 1]], -1)
    return jnp.concatenate([top, low], -2).reshape(TAPS * C, C)


def conv_rows(held, weight_ref, dilation, first, count):
    pieces = []
    for tap in range(TAPS):
        piece = held[pl.ds(first + (tap - HALF) * dilation, count)]
        pieces.append(piece.reshape(count * held.shape[1], C))
    total = jnp.dot(
        jnp.concatenate(pieces, 1), weight_ref[...], preferred_element_type=jnp.float32
    )
    return total.astype(jnp.bfloat16).reshape(count, held.shape[1], C)


def lat_first(info, own, edge, rest, near, far, gain, weight, *refs):
    outs, held = refs[:-1], refs[-1]
    member = info[0]
    rows = own.shape[1]
    other = 1 - member
    spare = rows - REACH

    def put(ref, at, state=None):
        value = ref[...]
        size = value.shape[0]
        if state is not None:
            state[pl.ds(at - REACH, size)] = value
        held[pl.ds(at, size)] = scaled(value.astype(jnp.float32), gain[...]).astype(jnp.bfloat16)

    def work(across, state):
        put(near, other * (REACH + 2 * rows))
        put(far, member * (REACH + 2 * rows))
        put(own.at[0], REACH + member * rows, state)
        put(edge, REACH + other * (rows + spare), state)
        put(rest, REACH + other * rows + member * REACH, state)
        for part in range(2):
            across[part * rows : (part + 1) * rows] = conv_rows(
                held, weight, info[1], REACH + part * rows, rows
            )

    if len(outs) == 2:
        work(*outs)
        return

    @pl.when(pl.program_id(0) == 0)
    def _():
        work(outs[0], outs[2])

    @pl.when(pl.program_id(0) == 1)
    def _():
        work(outs[1], outs[3])


def put_ends(across, head, tail):
    step = pl.program_id(0)

    @pl.when(step == 0)
    def _():
        head[...] = across[...]

    @pl.when(step == pl.num_programs(0) - 1)
    def _():
        tail[...] = across[...]


def lat_inner(info, top, bottom, inner, weight, across, head, tail, held):
    rows = inner.shape[0]
    held[0:REACH] = top[...]
    held[REACH : REACH + rows] = inner[...]
    held[REACH + rows : 2 * REACH + rows] = bottom[...]
    across[...] = conv_rows(held, weight, info[2], REACH, rows)
    put_ends(across, head, tail)


def lat_edge(info, top, bottom, inner, north, south, weight, across, head, tail, held):
    rows = inner.shape[0]
    at = 0
    for ref in (north, top, inner, bottom, south):
        held[at : at + ref.shape[0]] = ref[...]
        at += ref.shape[0]
    across[0:REACH] = conv_rows(held, weight, info[2], REACH, REACH)
    across[REACH:] = conv_rows(held, weight, info[2], 2 * REACH + rows, REACH)
    put_ends(across, head, tail)


def lon_total(dilation, pieces, weight, wide):
    at = 0
    for piece in pieces:
        width = piece.shape[1]
        for group in range(GROUPS):
            wide[group, :, at : at + width] = piece[
                :, :, group * CG : (group + 1) * CG
            ].astype(jnp.float32)
        at += width
    cols = at - 2 * LON_REACH
    totals = []
    for row in range(TILE_ROWS):
        taps = []
        for tap in range(TAPS):
            start = LON_REACH + (tap - HALF) * dilation
            for group in range(GROUPS):
                piece = wide[group, row, pl.ds(start, cols), :]
                taps.append(piece.astype(jnp.bfloat16))
        totals.append(
            jnp.dot(
                jnp.concatenate(taps, 1), weight[...], preferred_element_type=jnp.float32
            )
        )
    return totals


def lon_first(split, info, *refs):
    pieces, states = refs[:5], refs[5:8]
    ocean, gain, weight, state_out = refs[8:12]
    normed, wide = refs[12:-1], refs[-1]
    totals = lon_total(info[3], pieces, weight, wide)
    values = []
    for row, total in enumerate(totals):
        total = total * ocean[0][:, row : row + 1]
        old = jnp.concatenate([ref[row] for ref in states], 0)
        new = (old.astype(jnp.float32) + total).astype(jnp.bfloat16)
        state_out[row] = new
        values.append(scaled(new.astype(jnp.float32), gain[...]).astype(jnp.bfloat16))

    def put(ref):
        for row, value in enumerate(values):
            ref[row] = value

    if split:
        first = pl.program_id(0) < pl.num_programs(0) // 2
        pl.when(first)(lambda: put(normed[0]))
        pl.when(jnp.logical_not(first))(lambda: put(normed[1]))
    else:
        put(normed[0])


def lon_mlp(info, base, left, middle, right, state, ocean, gain, weight, w_in, w_out, out, wide):
    totals = lon_total(info[4], (left, middle, right), weight, wide)
    for row, total in enumerate(totals):
        old = state[row].astype(jnp.float32)
        new = (old + total * ocean[0][:, row : row + 1]).astype(jnp.bfloat16).astype(jnp.float32)
        lifted = scaled(new, gain[...]).astype(jnp.bfloat16)
        half = 0.5 * jnp.dot(lifted, w_in[...], preferred_element_type=jnp.float32)
        hidden = (half + half * jnp.tanh(half)).astype(jnp.bfloat16)
        update = jnp.dot(hidden, w_out[...], preferred_element_type=jnp.float32)
        out[row] = (new + update).astype(jnp.bfloat16)


def whole(array):
    dims = array.ndim
    return pl.BlockSpec(array.shape, lambda *_: (0,) * dims, pipeline_mode=pl.Buffered(1))


def launch(body, scalars, grid, specs, out_specs, out_shape, scratch, flops, args):
    moved = sum(s.size * 2 for s in jax.tree.leaves(out_shape)) * 2
    return pl.pallas_call(
        body,
        grid_spec=pltpu.PrefetchScalarGridSpec(
            num_scalar_prefetch=len(scalars),
            grid=(grid,),
            in_specs=specs,
            out_specs=out_specs,
            scratch_shapes=scratch,
        ),
        out_shape=out_shape,
        compiler_params=pltpu.CompilerParams(vmem_limit_bytes=VMEM_LIMIT),
        cost_estimate=pl.CostEstimate(flops=flops, bytes_accessed=moved, transcendentals=0),
    )(*scalars, *args)


def after(x, *others):
    return lax.optimization_barrier((x, *others))[0]


def on_device(
    fields,
    mix_gain,
    lat_weight,
    lon_weight,
    mlp_gain,
    w_in,
    w_out,
    lat_dilation,
    lon_dilation,
    ocean,
):
    bf16 = jnp.bfloat16
    rows, cols = fields.shape[1:3]
    spare = rows - REACH
    count = lax.axis_size("lat")
    around = lax.axis_size("lon")
    member = lax.rem(lax.axis_index("lat"), 2).astype(jnp.int32)
    other = 1 - member
    swap_pairs = [(i, i ^ 1) for i in range(count)]
    south_pairs = [(i, i + 2) for i in range(count - 2)]
    north_pairs = [(i + 2, i) for i in range(count - 2)]
    near_pairs = [p for p in north_pairs if p[0] % 2 == 0] + [p for p in south_pairs if p[0] % 2]
    far_pairs = [p for p in south_pairs if p[0] % 2 == 0] + [p for p in north_pairs if p[0] % 2]
    east_pairs = [(i, (i + 1) % around) for i in range(around)]
    west_pairs = [((i + 1) % around, i) for i in range(around)]

    def swap(x):
        return lax.ppermute(x, "lat", swap_pairs)

    def lon_halo(head, tail):
        return lax.ppermute(tail, "lon", east_pairs), lax.ppermute(head, "lon", west_pairs)

    def lat_flops(r, c):
        return 2 * r * c * TAPS * C * C

    def cut(sample, at, size):
        return lax.dynamic_slice(fields, (sample, at, 0, 0), (1, size, cols, C))[0]

    edge = swap(cut(other, member * spare, REACH))
    rest = swap(cut(other, other * REACH, spare))
    near = lax.ppermute(cut(member, member * spare, REACH), "lat", near_pairs)

    info = jnp.concatenate([member[None], lat_dilation, lon_dilation])
    send_edge_base = jnp.stack([other * (REACH // TILE_ROWS)])
    keep_edge_base = jnp.stack([member * (REACH // TILE_ROWS)])
    lat_w = [block_diagonal(lat_weight[l]) for l in range(LAYERS)]
    lon_w = [block_diagonal(lon_weight[l]) for l in range(LAYERS)]
    gains = [mix_gain[0:1], mix_gain[1:2], mlp_gain[None]]

    early = (info, send_edge_base, keep_edge_base, *lat_w, *lon_w, *gains)
    edge, info, send_edge_base, keep_edge_base, w0, w1, v0, v1, *gains = lax.optimization_barrier(
        (edge, *early)
    )
    lat_w, lon_w = (w0, w1), (v0, v1)
    far = lax.ppermute(edge, "lat", far_pairs)

    wet = after(ocean, edge).astype(jnp.float32)
    wet_came = swap(wet)
    wet = jnp.where(
        member == 0, jnp.concatenate([wet, wet_came], 0), jnp.concatenate([wet_came, wet], 0)
    )
    tiles = 2 * rows // TILE_ROWS
    wet = wet.reshape(tiles, TILE_ROWS, cols).transpose(0, 2, 1)
    rest = after(rest, wet)
    edge_tiles = REACH // TILE_ROWS
    inner_tiles = tiles - 2 * edge_tiles

    def edge_tile(i):
        return jnp.where(i < edge_tiles, i, i + inner_tiles)

    def inner_tile(i):
        return i + edge_tiles

    strips = cols // TILE_COLS
    one = jax.ShapeDtypeStruct((2 * rows, TILE_COLS, C), bf16)

    def first_lat(grid, place, out_specs, out_shape, rest):
        strip = lambda size: pl.BlockSpec((size, TILE_COLS, C), lambda i, s: (0, place(i), 0))
        return launch(
            lat_first,
            (info,),
            grid,
            [
                pl.BlockSpec((1, rows, TILE_COLS, C), lambda i, s: (s[0], 0, place(i), 0)),
                strip(REACH),
                strip(spare),
                strip(REACH),
                strip(REACH),
                whole(gains[0]),
                whole(lat_w[0]),
            ],
            out_specs,
            out_shape,
            [pltpu.VMEM((2 * rows + 2 * REACH, TILE_COLS, C), bf16)],
            lat_flops(2 * rows, grid * TILE_COLS),
            (fields, edge, rest, near, far, gains[0], lat_w[0]),
        )

    fixed = pl.BlockSpec((2 * rows, TILE_COLS, C), lambda i, s: (0, 0, 0))
    head, tail, state_head, state_tail = first_lat(
        2, lambda i: i * (strips - 1), [fixed] * 4, [one] * 4, rest
    )
    left, right = lon_halo(head, tail)
    inside = (strips - 2) * TILE_COLS
    middle, state_middle = first_lat(
        strips - 2,
        lambda i: i + 1,
        [pl.BlockSpec((2 * rows, TILE_COLS, C), lambda i, s: (0, i, 0))] * 2,
        [jax.ShapeDtypeStruct((2 * rows, inside, C), bf16)] * 2,
        after(rest, head),
    )
    wide = pltpu.VMEM((GROUPS, TILE_ROWS, cols + 2 * LON_REACH, CG), jnp.float32)

    def first_pair(split, to_tile):
        number = 2 * edge_tiles if split else inner_tiles
        half = edge_tiles
        band = lambda width: pl.BlockSpec((TILE_ROWS, width, C), lambda i, s: (to_tile(i), 0, 0))
        shape = lambda n: jax.ShapeDtypeStruct((n * TILE_ROWS, cols, C), bf16)
        block = (TILE_ROWS, cols, C)
        specs = [pl.BlockSpec(block, lambda i, s: (i, 0, 0))]
        shapes = [shape(number)]
        if split:
            specs.append(pl.BlockSpec(block, lambda i, s: (jnp.minimum(i, half - 1), 0, 0)))
            specs.append(pl.BlockSpec(block, lambda i, s: (jnp.maximum(i - half, 0), 0, 0)))
            shapes += [shape(half)] * 2
        else:
            specs.append(specs[0])
            shapes.append(shape(number))
        widths = (TILE_COLS, inside, TILE_COLS)
        return launch(
            functools.partial(lon_first, split),
            (info,),
            number,
            [band(n) for n in (LON_REACH, *widths, LON_REACH, *widths)]
            + [
                pl.BlockSpec((1, cols, TILE_ROWS), lambda i, s: (to_tile(i), 0, 0)),
                whole(gains[1]),
                whole(lon_w[0]),
            ],
            specs,
            shapes,
            [wide],
            lat_flops(number * TILE_ROWS, cols),
            (
                left,
                head,
                middle,
                tail,
                right,
                state_head,
                state_middle,
                state_tail,
                wet,
                gains[1],
                lon_w[0],
            ),
        )

    edge_state, top, bottom = first_pair(True, edge_tile)
    north = lax.ppermute(bottom, "lat", south_pairs)
    south = lax.ppermute(top, "lat", north_pairs)
    inner_state, inner_normed = first_pair(False, inner_tile)

    inner_rows = inner_state.shape[0]
    strip = lambda size: pl.BlockSpec((size, TILE_COLS, C), lambda i, s: (0, i, 0))

    def second_lat(body, out_rows, held_rows, args):
        end = pl.BlockSpec((out_rows, TILE_COLS, C), lambda i, s: (0, 0, 0))
        end_shape = jax.ShapeDtypeStruct((out_rows, TILE_COLS, C), bf16)
        return launch(
            body,
            (info,),
            strips,
            [strip(a.shape[0]) for a in args] + [whole(lat_w[1])],
            [strip(out_rows), end, end],
            [jax.ShapeDtypeStruct((out_rows, cols, C), bf16), end_shape, end_shape],
            [pltpu.VMEM((held_rows, TILE_COLS, C), bf16)],
            lat_flops(out_rows, cols),
            (*args, lat_w[1]),
        )

    inner_across, head, tail = second_lat(
        lat_inner, inner_rows, 2 * REACH + inner_rows, (top, bottom, inner_normed)
    )
    inner_halo = lon_halo(head, tail)

    def second(acr, halo, old, to_tile, base, number):
        band = lambda width: pl.BlockSpec((TILE_ROWS, width, C), lambda i, s, b: (b[0] + i, 0, 0))
        size = number * TILE_ROWS
        return launch(
            lon_mlp,
            (info, base),
            number,
            [
                band(LON_REACH),
                band(cols),
                band(LON_REACH),
                band(cols),
                pl.BlockSpec((1, cols, TILE_ROWS), lambda i, s, b: (to_tile(b[0] + i), 0, 0)),
                whole(gains[2]),
                whole(lon_w[1]),
                whole(w_in),
                whole(w_out),
            ],
            pl.BlockSpec((TILE_ROWS, cols, C), lambda i, s, b: (i, 0, 0)),
            jax.ShapeDtypeStruct((size, cols, C), bf16),
            [wide],
            lat_flops(size, cols) + 16 * size * cols * C * C,
            (halo[0], acr, halo[1], old, wet, gains[2], lon_w[1], w_in, w_out),
        )

    half_inner = inner_tiles // 2
    send_inner = second(
        inner_across, inner_halo, inner_state, inner_tile, send_edge_base, half_inner
    )
    back_inner = swap(send_inner)
    north = after(north, send_inner)
    edge_across, head, tail = second_lat(
        lat_edge, 2 * REACH, 4 * REACH + inner_rows, (top, bottom, inner_normed, north, south)
    )
    edge_halo = lon_halo(head, tail)
    send_edge = second(edge_across, edge_halo, edge_state, edge_tile, send_edge_base, edge_tiles)
    back_edge = swap(send_edge)
    keep_inner = second(
        after(inner_across, send_edge),
        inner_halo,
        inner_state,
        inner_tile,
        keep_edge_base,
        half_inner,
    )
    keep_edge = second(
        after(edge_across, send_edge), edge_halo, edge_state, edge_tile, keep_edge_base, edge_tiles
    )
    out = jnp.zeros(fields.shape, bf16)
    edge_at = member * spare
    inner_at = other * REACH
    for piece, sample, at in (
        (keep_inner, member, inner_at),
        (keep_edge, member, edge_at),
        (back_inner, other, inner_at),
        (back_edge, other, edge_at),
    ):
        out = lax.dynamic_update_slice(out, piece[None], (sample, at, 0, 0))
    return out


def solution(mesh):
    return jax.shard_map(
        on_device,
        mesh=mesh,
        in_specs=(
            P("grp", "lat", "lon", None),
            P(),
            P(),
            P(),
            P(),
            P(),
            P(),
            P(),
            P(),
            P(("grp", "lat"), "lon"),
        ),
        out_specs=P("grp", "lat", "lon", None),
        check_vma=False,
    )
```

```python
import functools

import jax
import jax.numpy as jnp
from jax import lax
from jax.experimental import pallas as pl
from jax.experimental.pallas import tpu as pltpu
from jax.sharding import PartitionSpec as P

C = 256
GROUPS = 2
CG = 128
TAPS = 5
HALF = 2
LAYERS = 2
MAXDIL_LAT = 4
MAXDIL_LON = 24
REACH = HALF * MAXDIL_LAT
LON_REACH = HALF * MAXDIL_LON
TILE_COLS = LON_REACH
TILE_ROWS = 4
COST_SHARE = 100000000
VMEM_LIMIT = 48 * 1024 * 1024


def scaled(wide, gain):
    power = jnp.mean(wide * wide, axis=-1, keepdims=True)
    return wide * lax.rsqrt(power + 1e-06) * gain


def block_diagonal(weight):
    zero = jnp.zeros_like(weight[:, 0])
    top = jnp.concatenate([weight[:, 0], zero], -1)
    low = jnp.concatenate([zero, weight[:, 1]], -1)
    return jnp.concatenate([top, low], -2).reshape(TAPS * C, C)


def conv_rows(held, weight_ref, dilation, first, count):
    pieces = []
    for tap in range(TAPS):
        piece = held[pl.ds(first + (tap - HALF) * dilation, count)]
        pieces.append(piece.reshape(count * held.shape[1], C))
    total = jnp.dot(
        jnp.concatenate(pieces, 1), weight_ref[...], preferred_element_type=jnp.float32
    )
    return total.astype(jnp.bfloat16).reshape(count, held.shape[1], C)


def lat_first(info, own, edge, rest, near, far, gain, weight, *refs):
    outs, held = refs[:-1], refs[-1]
    member = info[0]
    rows = own.shape[1]
    other = 1 - member
    spare = rows - REACH

    def put(ref, at, state=None):
        value = ref[...]
        size = value.shape[0]
        if state is not None:
            state[pl.ds(at - REACH, size)] = value
        held[pl.ds(at, size)] = scaled(value.astype(jnp.float32), gain[...]).astype(jnp.bfloat16)

    def work(across, state):
        put(near, other * (REACH + 2 * rows))
        put(far, member * (REACH + 2 * rows))
        put(own.at[0], REACH + member * rows, state)
        put(edge, REACH + other * (rows + spare), state)
        put(rest, REACH + other * rows + member * REACH, state)
        for part in range(2):
            across[part * rows : (part + 1) * rows] = conv_rows(
                held, weight, info[1], REACH + part * rows, rows
            )

    if len(outs) == 2:
        work(*outs)
        return

    @pl.when(pl.program_id(0) == 0)
    def _():
        work(outs[0], outs[2])

    @pl.when(pl.program_id(0) == 1)
    def _():
        work(outs[1], outs[3])


def put_ends(across, head, tail):
    step = pl.program_id(0)

    @pl.when(step == 0)
    def _():
        head[...] = across[...]

    @pl.when(step == pl.num_programs(0) - 1)
    def _():
        tail[...] = across[...]


def lat_inner(info, top, bottom, inner, weight, across, head, tail, held):
    rows = inner.shape[0]
    held[0:REACH] = top[...]
    held[REACH : REACH + rows] = inner[...]
    held[REACH + rows : 2 * REACH + rows] = bottom[...]
    first = REACH + (1 - info[0]) * across.shape[0]
    across[...] = conv_rows(held, weight, info[2], first, across.shape[0])
    put_ends(across, head, tail)


def lat_others(info, top, bottom, inner, north, south, weight, across, head, tail, held):
    rows = inner.shape[0]
    at = 0
    for ref in (north, top, inner, bottom, south):
        held[at : at + ref.shape[0]] = ref[...]
        at += ref.shape[0]
    half = rows // 2
    across[0:REACH] = conv_rows(held, weight, info[2], REACH, REACH)
    across[REACH : 2 * REACH] = conv_rows(held, weight, info[2], 2 * REACH + rows, REACH)
    across[2 * REACH :] = conv_rows(held, weight, info[2], 2 * REACH + info[0] * half, half)
    put_ends(across, head, tail)


def lon_total(dilation, pieces, weight, wide):
    at = 0
    for piece in pieces:
        width = piece.shape[1]
        for group in range(GROUPS):
            wide[group, :, at : at + width] = piece[
                :, :, group * CG : (group + 1) * CG
            ].astype(jnp.float32)
        at += width
    cols = at - 2 * LON_REACH
    taps = []
    for tap in range(TAPS):
        start = LON_REACH + (tap - HALF) * dilation
        for group in range(GROUPS):
            piece = wide[group, :, pl.ds(start, cols), :]
            taps.append(piece.astype(jnp.bfloat16).reshape(TILE_ROWS * cols, CG))
    total = jnp.dot(
        jnp.concatenate(taps, 1), weight[...], preferred_element_type=jnp.float32
    )
    return [total[row * cols : (row + 1) * cols] for row in range(TILE_ROWS)]


def lon_first(split, info, *refs):
    pieces, states = refs[:5], refs[5:8]
    ocean, gain, weight, state_out = refs[8:12]
    normed, wide = refs[12:-1], refs[-1]
    totals = lon_total(info[3], pieces, weight, wide)
    values = []
    for row, total in enumerate(totals):
        total = total * ocean[0][:, row : row + 1]
        old = jnp.concatenate([ref[row] for ref in states], 0)
        new = (old.astype(jnp.float32) + total).astype(jnp.bfloat16)
        state_out[row] = new
        values.append(scaled(new.astype(jnp.float32), gain[...]).astype(jnp.bfloat16))

    def put(ref):
        for row, value in enumerate(values):
            ref[row] = value

    if split:
        first = pl.program_id(0) < pl.num_programs(0) // 2
        pl.when(first)(lambda: put(normed[0]))
        pl.when(jnp.logical_not(first))(lambda: put(normed[1]))
    else:
        put(normed[0])


def lon_mlp(info, base, left, middle, right, state, ocean, gain, weight, w_in, w_out, out, wide):
    totals = lon_total(info[4], (left, middle, right), weight, wide)
    for row, total in enumerate(totals):
        old = state[row].astype(jnp.float32)
        new = (old + total * ocean[0][:, row : row + 1]).astype(jnp.bfloat16).astype(jnp.float32)
        lifted = scaled(new, gain[...]).astype(jnp.bfloat16)
        half = 0.5 * jnp.dot(lifted, w_in[...], preferred_element_type=jnp.float32)
        hidden = (half + half * jnp.tanh(half)).astype(jnp.bfloat16)
        update = jnp.dot(hidden, w_out[...], preferred_element_type=jnp.float32)
        out[row] = (new + update).astype(jnp.bfloat16)


def whole(array):
    dims = array.ndim
    return pl.BlockSpec(array.shape, lambda *_: (0,) * dims, pipeline_mode=pl.Buffered(1))


def launch(body, scalars, grid, specs, out_specs, out_shape, scratch, flops, args):
    moved = sum(s.size * 2 for s in jax.tree.leaves(out_shape)) * 2
    return pl.pallas_call(
        body,
        grid_spec=pltpu.PrefetchScalarGridSpec(
            num_scalar_prefetch=len(scalars),
            grid=(grid,),
            in_specs=specs,
            out_specs=out_specs,
            scratch_shapes=scratch,
        ),
        out_shape=out_shape,
        compiler_params=pltpu.CompilerParams(vmem_limit_bytes=VMEM_LIMIT),
        cost_estimate=pl.CostEstimate(flops=flops // COST_SHARE, bytes_accessed=moved // COST_SHARE, transcendentals=0),
    )(*scalars, *args)


def after(x, *others):
    return lax.optimization_barrier((x, *others))[0]


def on_device(
    fields,
    mix_gain,
    lat_weight,
    lon_weight,
    mlp_gain,
    w_in,
    w_out,
    lat_dilation,
    lon_dilation,
    ocean,
):
    bf16 = jnp.bfloat16
    rows, cols = fields.shape[1:3]
    spare = rows - REACH
    count = lax.axis_size("lat")
    around = lax.axis_size("lon")
    member = lax.rem(lax.axis_index("lat"), 2).astype(jnp.int32)
    other = 1 - member
    swap_pairs = [(i, i ^ 1) for i in range(count)]
    south_pairs = [(i, i + 2) for i in range(count - 2)]
    north_pairs = [(i + 2, i) for i in range(count - 2)]
    near_pairs = [p for p in north_pairs if p[0] % 2 == 0] + [p for p in south_pairs if p[0] % 2]
    far_pairs = [p for p in south_pairs if p[0] % 2 == 0] + [p for p in north_pairs if p[0] % 2]
    east_pairs = [(i, (i + 1) % around) for i in range(around)]
    west_pairs = [((i + 1) % around, i) for i in range(around)]

    def swap(x):
        return lax.ppermute(x, "lat", swap_pairs)

    def lon_halo(head, tail):
        return lax.ppermute(tail, "lon", east_pairs), lax.ppermute(head, "lon", west_pairs)

    def lat_flops(r, c):
        return 2 * r * c * TAPS * C * C

    def cut(sample, at, size):
        return lax.dynamic_slice(fields, (sample, at, 0, 0), (1, size, cols, C))[0]

    edge_piece = cut(other, member * spare, REACH)
    edge = swap(edge_piece)
    whole_fields = fields
    fields = after(fields, edge_piece)
    rest = swap(cut(other, other * REACH, spare))
    near = lax.ppermute(cut(member, member * spare, REACH), "lat", near_pairs)

    info = jnp.concatenate([member[None], lat_dilation, lon_dilation])
    edge_tiles = REACH // TILE_ROWS
    half_inner = spare // TILE_ROWS
    bases = [
        jnp.stack([jnp.int32(0), other * half_inner]),
        jnp.stack([other * edge_tiles, other * edge_tiles]),
        jnp.stack([member * edge_tiles, member * edge_tiles]),
        jnp.stack([jnp.int32(2 * edge_tiles), member * half_inner]),
    ]
    lat_w = [block_diagonal(lat_weight[l]) for l in range(LAYERS)]
    lon_w = [block_diagonal(lon_weight[l]) for l in range(LAYERS)]
    gains = [mix_gain[0:1], mix_gain[1:2], mlp_gain[None]]

    early = (info, *bases, *lat_w, *lon_w, *gains)
    edge, info, *early = lax.optimization_barrier((edge, *early))
    bases, (w0, w1, v0, v1), gains = early[:4], early[4:8], early[8:]
    lat_w, lon_w = (w0, w1), (v0, v1)
    far = lax.ppermute(edge, "lat", far_pairs)

    wet = after(ocean, edge).astype(jnp.float32)
    wet_came = swap(wet)
    wet = jnp.where(
        member == 0, jnp.concatenate([wet, wet_came], 0), jnp.concatenate([wet_came, wet], 0)
    )
    tiles = 2 * rows // TILE_ROWS
    wet = wet.reshape(tiles, TILE_ROWS, cols).transpose(0, 2, 1)
    rest = after(rest, wet)
    inner_tiles = tiles - 2 * edge_tiles

    def edge_tile(i):
        return jnp.where(i < edge_tiles, i, i + inner_tiles)

    def inner_tile(i):
        return i + edge_tiles

    strips = cols // TILE_COLS
    one = jax.ShapeDtypeStruct((2 * rows, TILE_COLS, C), bf16)

    def first_lat(grid, place, out_specs, out_shape, rest):
        strip = lambda size: pl.BlockSpec((size, TILE_COLS, C), lambda i, s: (0, place(i), 0))
        return launch(
            lat_first,
            (info,),
            grid,
            [
                pl.BlockSpec((1, rows, TILE_COLS, C), lambda i, s: (s[0], 0, place(i), 0)),
                strip(REACH),
                strip(spare),
                strip(REACH),
                strip(REACH),
                whole(gains[0]),
                whole(lat_w[0]),
            ],
            out_specs,
            out_shape,
            [pltpu.VMEM((2 * rows + 2 * REACH, TILE_COLS, C), bf16)],
            lat_flops(2 * rows, grid * TILE_COLS),
            (whole_fields, edge, rest, near, far, gains[0], lat_w[0]),
        )

    fixed = pl.BlockSpec((2 * rows, TILE_COLS, C), lambda i, s: (0, 0, 0))
    head, tail, state_head, state_tail = first_lat(
        2, lambda i: i * (strips - 1), [fixed] * 4, [one] * 4, rest
    )
    left, right = lon_halo(head, tail)
    inside = (strips - 2) * TILE_COLS
    middle, state_middle = first_lat(
        strips - 2,
        lambda i: i + 1,
        [pl.BlockSpec((2 * rows, TILE_COLS, C), lambda i, s: (0, i, 0))] * 2,
        [jax.ShapeDtypeStruct((2 * rows, inside, C), bf16)] * 2,
        after(rest, head),
    )
    wide = pltpu.VMEM((GROUPS, TILE_ROWS, cols + 2 * LON_REACH, CG), jnp.float32)

    def first_pair(split, to_tile):
        number = 2 * edge_tiles if split else inner_tiles
        half = edge_tiles
        band = lambda width: pl.BlockSpec((TILE_ROWS, width, C), lambda i, s: (to_tile(i), 0, 0))
        shape = lambda n: jax.ShapeDtypeStruct((n * TILE_ROWS, cols, C), bf16)
        block = (TILE_ROWS, cols, C)
        specs = [pl.BlockSpec(block, lambda i, s: (i, 0, 0))]
        shapes = [shape(number)]
        if split:
            specs.append(pl.BlockSpec(block, lambda i, s: (jnp.minimum(i, half - 1), 0, 0)))
            specs.append(pl.BlockSpec(block, lambda i, s: (jnp.maximum(i - half, 0), 0, 0)))
            shapes += [shape(half)] * 2
        else:
            specs.append(specs[0])
            shapes.append(shape(number))
        widths = (TILE_COLS, inside, TILE_COLS)
        return launch(
            functools.partial(lon_first, split),
            (info,),
            number,
            [band(n) for n in (LON_REACH, *widths, LON_REACH, *widths)]
            + [
                pl.BlockSpec((1, cols, TILE_ROWS), lambda i, s: (to_tile(i), 0, 0)),
                whole(gains[1]),
                whole(lon_w[0]),
            ],
            specs,
            shapes,
            [wide],
            lat_flops(number * TILE_ROWS, cols),
            (
                left,
                head,
                middle,
                tail,
                right,
                state_head,
                state_middle,
                state_tail,
                wet,
                gains[1],
                lon_w[0],
            ),
        )

    edge_state, top, bottom = first_pair(True, edge_tile)
    north = lax.ppermute(bottom, "lat", south_pairs)
    south = lax.ppermute(top, "lat", north_pairs)
    inner_state, inner_normed = first_pair(False, inner_tile)

    inner_rows = inner_state.shape[0]
    strip = lambda size: pl.BlockSpec((size, TILE_COLS, C), lambda i, s: (0, i, 0))

    def second_lat(body, out_rows, held_rows, args):
        end = pl.BlockSpec((out_rows, TILE_COLS, C), lambda i, s: (0, 0, 0))
        end_shape = jax.ShapeDtypeStruct((out_rows, TILE_COLS, C), bf16)
        return launch(
            body,
            (info,),
            strips,
            [strip(a.shape[0]) for a in args] + [whole(lat_w[1])],
            [strip(out_rows), end, end],
            [jax.ShapeDtypeStruct((out_rows, cols, C), bf16), end_shape, end_shape],
            [pltpu.VMEM((held_rows, TILE_COLS, C), bf16)],
            lat_flops(out_rows, cols),
            (*args, lat_w[1]),
        )

    lon_rows = inner_rows // 2
    inner_across, head, tail = second_lat(
        lat_inner, lon_rows, 2 * REACH + inner_rows, (top, bottom, inner_normed)
    )
    inner_halo = lon_halo(head, tail)

    def second(acr, halo, old, to_tile, base, number):
        band = lambda width, which: pl.BlockSpec(
            (TILE_ROWS, width, C), lambda i, s, b: (b[which] + i, 0, 0)
        )
        size = number * TILE_ROWS
        return launch(
            lon_mlp,
            (info, base),
            number,
            [
                band(LON_REACH, 0),
                band(cols, 0),
                band(LON_REACH, 0),
                band(cols, 1),
                pl.BlockSpec((1, cols, TILE_ROWS), lambda i, s, b: (to_tile(b[1] + i), 0, 0)),
                whole(gains[2]),
                whole(lon_w[1]),
                whole(w_in),
                whole(w_out),
            ],
            pl.BlockSpec((TILE_ROWS, cols, C), lambda i, s, b: (i, 0, 0)),
            jax.ShapeDtypeStruct((size, cols, C), bf16),
            [wide],
            lat_flops(size, cols) + 16 * size * cols * C * C,
            (halo[0], acr, halo[1], old, wet, gains[2], lon_w[1], w_in, w_out),
        )

    send_inner = second(
        inner_across, inner_halo, inner_state, inner_tile, bases[0], half_inner
    )
    back_inner = swap(send_inner)
    north = after(north, send_inner)
    edge_across, head, tail = second_lat(
        lat_others,
        2 * REACH + lon_rows,
        4 * REACH + inner_rows,
        (top, bottom, inner_normed, north, south),
    )
    edge_halo = lon_halo(head, tail)
    send_edge = second(edge_across, edge_halo, edge_state, edge_tile, bases[1], edge_tiles)
    back_edge = swap(send_edge)
    edge_across = after(edge_across, send_edge, back_inner)
    keep_inner = second(edge_across, edge_halo, inner_state, inner_tile, bases[3], half_inner)
    keep_edge = second(edge_across, edge_halo, edge_state, edge_tile, bases[2], edge_tiles)
    out = jnp.zeros(fields.shape, bf16)
    edge_at = member * spare
    inner_at = other * REACH
    for piece, sample, at in (
        (keep_inner, member, inner_at),
        (keep_edge, member, edge_at),
        (back_inner, other, inner_at),
        (back_edge, other, edge_at),
    ):
        out = lax.dynamic_update_slice(out, piece[None], (sample, at, 0, 0))
    return out


def solution(mesh):
    return jax.shard_map(
        on_device,
        mesh=mesh,
        in_specs=(
            P("grp", "lat", "lon", None),
            P(),
            P(),
            P(),
            P(),
            P(),
            P(),
            P(),
            P(),
            P(("grp", "lat"), "lon"),
        ),
        out_specs=P("grp", "lat", "lon", None),
        check_vma=False,
    )
```

```python
import functools

import jax
import jax.numpy as jnp
from jax import lax
from jax.experimental import pallas as pl
from jax.experimental.pallas import tpu as pltpu
from jax.sharding import PartitionSpec as P

C = 256
GROUPS = 2
CG = 128
TAPS = 5
HALF = 2
LAYERS = 2
MAXDIL_LAT = 4
MAXDIL_LON = 24
REACH = HALF * MAXDIL_LAT
LON_REACH = HALF * MAXDIL_LON
TILE_COLS = LON_REACH
TILE_ROWS = 4
COST_SHARE = 100000000
VMEM_LIMIT = 48 * 1024 * 1024


def scaled(wide, gain):
    power = jnp.mean(wide * wide, axis=-1, keepdims=True)
    return wide * lax.rsqrt(power + 1e-06) * gain


def block_diagonal(weight):
    zero = jnp.zeros_like(weight[:, 0])
    top = jnp.concatenate([weight[:, 0], zero], -1)
    low = jnp.concatenate([zero, weight[:, 1]], -1)
    return jnp.concatenate([top, low], -2).reshape(TAPS * C, C)


def conv_rows(held, weight_ref, dilation, first, count):
    pieces = []
    for tap in range(TAPS):
        piece = held[pl.ds(first + (tap - HALF) * dilation, count)]
        pieces.append(piece.reshape(count * held.shape[1], C))
    total = jnp.dot(
        jnp.concatenate(pieces, 1), weight_ref[...], preferred_element_type=jnp.float32
    )
    return total.astype(jnp.bfloat16).reshape(count, held.shape[1], C)


def lat_first(info, own, edge, rest, near, far, gain, weight, *refs):
    outs, held = refs[:-1], refs[-1]
    member = info[0]
    rows = own.shape[1]
    other = 1 - member
    spare = rows - REACH

    def put(ref, at, state=None):
        value = ref[...]
        size = value.shape[0]
        if state is not None:
            state[pl.ds(at - REACH, size)] = value
        held[pl.ds(at, size)] = scaled(value.astype(jnp.float32), gain[...]).astype(jnp.bfloat16)

    def work(across, state):
        put(near, other * (REACH + 2 * rows))
        put(far, member * (REACH + 2 * rows))
        put(own.at[0], REACH + member * rows, state)
        put(edge, REACH + other * (rows + spare), state)
        put(rest, REACH + other * rows + member * REACH, state)
        for part in range(2):
            across[part * rows : (part + 1) * rows] = conv_rows(
                held, weight, info[1], REACH + part * rows, rows
            )

    if len(outs) == 2:
        work(*outs)
        return

    @pl.when(pl.program_id(0) == 0)
    def _():
        work(outs[0], outs[2])

    @pl.when(pl.program_id(0) == 1)
    def _():
        work(outs[1], outs[3])


def put_ends(across, head, tail):
    step = pl.program_id(0)

    @pl.when(step == 0)
    def _():
        head[...] = across[...]

    @pl.when(step == pl.num_programs(0) - 1)
    def _():
        tail[...] = across[...]


def lat_inner(info, top, bottom, inner, weight, across, head, tail, held):
    rows = inner.shape[0]
    held[0:REACH] = top[...]
    held[REACH : REACH + rows] = inner[...]
    held[REACH + rows : 2 * REACH + rows] = bottom[...]
    first = REACH + (1 - info[0]) * across.shape[0]
    across[...] = conv_rows(held, weight, info[2], first, across.shape[0])
    put_ends(across, head, tail)


def lat_others(info, top, bottom, inner, north, south, weight, across, head, tail, held):
    rows = inner.shape[0]
    at = 0
    for ref in (north, top, inner, bottom, south):
        held[at : at + ref.shape[0]] = ref[...]
        at += ref.shape[0]
    half = rows // 2
    across[0:REACH] = conv_rows(held, weight, info[2], REACH, REACH)
    across[REACH : 2 * REACH] = conv_rows(held, weight, info[2], 2 * REACH + rows, REACH)
    across[2 * REACH :] = conv_rows(held, weight, info[2], 2 * REACH + info[0] * half, half)
    put_ends(across, head, tail)


def lon_total(dilation, pieces, weight, wide, by_row=False):
    at = 0
    for piece in pieces:
        width = piece.shape[1]
        for group in range(GROUPS):
            wide[group, :, at : at + width] = piece[
                :, :, group * CG : (group + 1) * CG
            ].astype(jnp.float32)
        at += width
    cols = at - 2 * LON_REACH
    if by_row:
        totals = []
        for row in range(TILE_ROWS):
            taps = []
            for tap in range(TAPS):
                start = LON_REACH + (tap - HALF) * dilation
                for group in range(GROUPS):
                    taps.append(wide[group, row, pl.ds(start, cols), :].astype(jnp.bfloat16))
            lhs = jnp.concatenate(taps, 1)
            totals.append(jnp.dot(lhs, weight[...], preferred_element_type=jnp.float32))
        return totals
    taps = []
    for tap in range(TAPS):
        start = LON_REACH + (tap - HALF) * dilation
        for group in range(GROUPS):
            piece = wide[group, :, pl.ds(start, cols), :]
            taps.append(piece.astype(jnp.bfloat16).reshape(TILE_ROWS * cols, CG))
    total = jnp.dot(
        jnp.concatenate(taps, 1), weight[...], preferred_element_type=jnp.float32
    )
    return [total[row * cols : (row + 1) * cols] for row in range(TILE_ROWS)]


def lon_first(split, info, *refs):
    pieces, states = refs[:5], refs[5:8]
    ocean, gain, weight, state_out = refs[8:12]
    normed, wide = refs[12:-1], refs[-1]
    totals = lon_total(info[3], pieces, weight, wide)
    values = []
    for row, total in enumerate(totals):
        total = total * ocean[0][:, row : row + 1]
        old = jnp.concatenate([ref[row] for ref in states], 0)
        new = (old.astype(jnp.float32) + total).astype(jnp.bfloat16)
        state_out[row] = new
        values.append(scaled(new.astype(jnp.float32), gain[...]).astype(jnp.bfloat16))

    def put(ref):
        for row, value in enumerate(values):
            ref[row] = value

    if split:
        first = pl.program_id(0) < pl.num_programs(0) // 2
        pl.when(first)(lambda: put(normed[0]))
        pl.when(jnp.logical_not(first))(lambda: put(normed[1]))
    else:
        put(normed[0])


def lon_mlp(info, base, left, middle, right, state, ocean, gain, weight, w_in, w_out, out, wide):
    totals = lon_total(info[4], (left, middle, right), weight, wide, True)
    for row, total in enumerate(totals):
        old = state[row].astype(jnp.float32)
        new = (old + total * ocean[0][:, row : row + 1]).astype(jnp.bfloat16).astype(jnp.float32)
        lifted = scaled(new, gain[...]).astype(jnp.bfloat16)
        half = 0.5 * jnp.dot(lifted, w_in[...], preferred_element_type=jnp.float32)
        hidden = (half + half * jnp.tanh(half)).astype(jnp.bfloat16)
        update = jnp.dot(hidden, w_out[...], preferred_element_type=jnp.float32)
        out[row] = (new + update).astype(jnp.bfloat16)


def whole(array):
    dims = array.ndim
    return pl.BlockSpec(array.shape, lambda *_: (0,) * dims, pipeline_mode=pl.Buffered(1))


def launch(body, scalars, grid, specs, out_specs, out_shape, scratch, flops, args):
    moved = sum(s.size * 2 for s in jax.tree.leaves(out_shape)) * 2
    return pl.pallas_call(
        body,
        grid_spec=pltpu.PrefetchScalarGridSpec(
            num_scalar_prefetch=len(scalars),
            grid=(grid,),
            in_specs=specs,
            out_specs=out_specs,
            scratch_shapes=scratch,
        ),
        out_shape=out_shape,
        compiler_params=pltpu.CompilerParams(vmem_limit_bytes=VMEM_LIMIT),
        cost_estimate=pl.CostEstimate(flops=flops // COST_SHARE, bytes_accessed=moved // COST_SHARE, transcendentals=0),
    )(*scalars, *args)


def after(x, *others):
    return lax.optimization_barrier((x, *others))[0]


def on_device(
    fields,
    mix_gain,
    lat_weight,
    lon_weight,
    mlp_gain,
    w_in,
    w_out,
    lat_dilation,
    lon_dilation,
    ocean,
):
    bf16 = jnp.bfloat16
    rows, cols = fields.shape[1:3]
    spare = rows - REACH
    count = lax.axis_size("lat")
    around = lax.axis_size("lon")
    member = lax.rem(lax.axis_index("lat"), 2).astype(jnp.int32)
    other = 1 - member
    swap_pairs = [(i, i ^ 1) for i in range(count)]
    south_pairs = [(i, i + 2) for i in range(count - 2)]
    north_pairs = [(i + 2, i) for i in range(count - 2)]
    near_pairs = [p for p in north_pairs if p[0] % 2 == 0] + [p for p in south_pairs if p[0] % 2]
    far_pairs = [p for p in south_pairs if p[0] % 2 == 0] + [p for p in north_pairs if p[0] % 2]
    east_pairs = [(i, (i + 1) % around) for i in range(around)]
    west_pairs = [((i + 1) % around, i) for i in range(around)]

    def swap(x):
        return lax.ppermute(x, "lat", swap_pairs)

    def lon_halo(head, tail):
        return lax.ppermute(tail, "lon", east_pairs), lax.ppermute(head, "lon", west_pairs)

    def lat_flops(r, c):
        return 2 * r * c * TAPS * C * C

    def cut(sample, at, size):
        return lax.dynamic_slice(fields, (sample, at, 0, 0), (1, size, cols, C))[0]

    edge_piece = cut(other, member * spare, REACH)
    edge = swap(edge_piece)
    whole_fields = fields
    fields = after(fields, edge_piece)
    rest = swap(cut(other, other * REACH, spare))
    near = lax.ppermute(cut(member, member * spare, REACH), "lat", near_pairs)

    info = jnp.concatenate([member[None], lat_dilation, lon_dilation])
    edge_tiles = REACH // TILE_ROWS
    half_inner = spare // TILE_ROWS
    bases = [
        jnp.stack([jnp.int32(0), other * half_inner]),
        jnp.stack([other * edge_tiles, other * edge_tiles]),
        jnp.stack([member * edge_tiles, member * edge_tiles]),
        jnp.stack([jnp.int32(2 * edge_tiles), member * half_inner]),
    ]
    lat_w = [block_diagonal(lat_weight[l]) for l in range(LAYERS)]
    lon_w = [block_diagonal(lon_weight[l]) for l in range(LAYERS)]
    gains = [mix_gain[0:1], mix_gain[1:2], mlp_gain[None]]

    early = (info, *bases, *lat_w, *lon_w, *gains)
    edge, info, *early = lax.optimization_barrier((edge, *early))
    bases, (w0, w1, v0, v1), gains = early[:4], early[4:8], early[8:]
    lat_w, lon_w = (w0, w1), (v0, v1)
    far = lax.ppermute(edge, "lat", far_pairs)

    wet = after(ocean, edge).astype(jnp.float32)
    wet_came = swap(wet)
    wet = jnp.where(
        member == 0, jnp.concatenate([wet, wet_came], 0), jnp.concatenate([wet_came, wet], 0)
    )
    tiles = 2 * rows // TILE_ROWS
    wet = wet.reshape(tiles, TILE_ROWS, cols).transpose(0, 2, 1)
    rest = after(rest, wet)
    inner_tiles = tiles - 2 * edge_tiles

    def edge_tile(i):
        return jnp.where(i < edge_tiles, i, i + inner_tiles)

    def inner_tile(i):
        return i + edge_tiles

    strips = cols // TILE_COLS
    one = jax.ShapeDtypeStruct((2 * rows, TILE_COLS, C), bf16)

    def first_lat(grid, place, out_specs, out_shape, rest):
        strip = lambda size: pl.BlockSpec((size, TILE_COLS, C), lambda i, s: (0, place(i), 0))
        return launch(
            lat_first,
            (info,),
            grid,
            [
                pl.BlockSpec((1, rows, TILE_COLS, C), lambda i, s: (s[0], 0, place(i), 0)),
                strip(REACH),
                strip(spare),
                strip(REACH),
                strip(REACH),
                whole(gains[0]),
                whole(lat_w[0]),
            ],
            out_specs,
            out_shape,
            [pltpu.VMEM((2 * rows + 2 * REACH, TILE_COLS, C), bf16)],
            lat_flops(2 * rows, grid * TILE_COLS),
            (whole_fields, edge, rest, near, far, gains[0], lat_w[0]),
        )

    fixed = pl.BlockSpec((2 * rows, TILE_COLS, C), lambda i, s: (0, 0, 0))
    head, tail, state_head, state_tail = first_lat(
        2, lambda i: i * (strips - 1), [fixed] * 4, [one] * 4, rest
    )
    left, right = lon_halo(head, tail)
    inside = (strips - 2) * TILE_COLS
    middle, state_middle = first_lat(
        strips - 2,
        lambda i: i + 1,
        [pl.BlockSpec((2 * rows, TILE_COLS, C), lambda i, s: (0, i, 0))] * 2,
        [jax.ShapeDtypeStruct((2 * rows, inside, C), bf16)] * 2,
        after(rest, head),
    )
    wide = pltpu.VMEM((GROUPS, TILE_ROWS, cols + 2 * LON_REACH, CG), jnp.float32)

    def first_pair(split, to_tile):
        number = 2 * edge_tiles if split else inner_tiles
        half = edge_tiles
        band = lambda width: pl.BlockSpec((TILE_ROWS, width, C), lambda i, s: (to_tile(i), 0, 0))
        shape = lambda n: jax.ShapeDtypeStruct((n * TILE_ROWS, cols, C), bf16)
        block = (TILE_ROWS, cols, C)
        specs = [pl.BlockSpec(block, lambda i, s: (i, 0, 0))]
        shapes = [shape(number)]
        if split:
            specs.append(pl.BlockSpec(block, lambda i, s: (jnp.minimum(i, half - 1), 0, 0)))
            specs.append(pl.BlockSpec(block, lambda i, s: (jnp.maximum(i - half, 0), 0, 0)))
            shapes += [shape(half)] * 2
        else:
            specs.append(specs[0])
            shapes.append(shape(number))
        widths = (TILE_COLS, inside, TILE_COLS)
        return launch(
            functools.partial(lon_first, split),
            (info,),
            number,
            [band(n) for n in (LON_REACH, *widths, LON_REACH, *widths)]
            + [
                pl.BlockSpec((1, cols, TILE_ROWS), lambda i, s: (to_tile(i), 0, 0)),
                whole(gains[1]),
                whole(lon_w[0]),
            ],
            specs,
            shapes,
            [wide],
            lat_flops(number * TILE_ROWS, cols),
            (
                left,
                head,
                middle,
                tail,
                right,
                state_head,
                state_middle,
                state_tail,
                wet,
                gains[1],
                lon_w[0],
            ),
        )

    edge_state, top, bottom = first_pair(True, edge_tile)
    north = lax.ppermute(bottom, "lat", south_pairs)
    south = lax.ppermute(top, "lat", north_pairs)
    inner_state, inner_normed = first_pair(False, inner_tile)

    inner_rows = inner_state.shape[0]
    strip = lambda size: pl.BlockSpec((size, TILE_COLS, C), lambda i, s: (0, i, 0))

    def second_lat(body, out_rows, held_rows, args):
        end = pl.BlockSpec((out_rows, TILE_COLS, C), lambda i, s: (0, 0, 0))
        end_shape = jax.ShapeDtypeStruct((out_rows, TILE_COLS, C), bf16)
        return launch(
            body,
            (info,),
            strips,
            [strip(a.shape[0]) for a in args] + [whole(lat_w[1])],
            [strip(out_rows), end, end],
            [jax.ShapeDtypeStruct((out_rows, cols, C), bf16), end_shape, end_shape],
            [pltpu.VMEM((held_rows, TILE_COLS, C), bf16)],
            lat_flops(out_rows, cols),
            (*args, lat_w[1]),
        )

    lon_rows = inner_rows // 2
    inner_across, head, tail = second_lat(
        lat_inner, lon_rows, 2 * REACH + inner_rows, (top, bottom, inner_normed)
    )
    inner_halo = lon_halo(head, tail)

    def second(acr, halo, old, to_tile, base, number):
        band = lambda width, which: pl.BlockSpec(
            (TILE_ROWS, width, C), lambda i, s, b: (b[which] + i, 0, 0)
        )
        size = number * TILE_ROWS
        return launch(
            lon_mlp,
            (info, base),
            number,
            [
                band(LON_REACH, 0),
                band(cols, 0),
                band(LON_REACH, 0),
                band(cols, 1),
                pl.BlockSpec((1, cols, TILE_ROWS), lambda i, s, b: (to_tile(b[1] + i), 0, 0)),
                whole(gains[2]),
                whole(lon_w[1]),
                whole(w_in),
                whole(w_out),
            ],
            pl.BlockSpec((TILE_ROWS, cols, C), lambda i, s, b: (i, 0, 0)),
            jax.ShapeDtypeStruct((size, cols, C), bf16),
            [wide],
            lat_flops(size, cols) + 16 * size * cols * C * C,
            (halo[0], acr, halo[1], old, wet, gains[2], lon_w[1], w_in, w_out),
        )

    send_inner = second(
        inner_across, inner_halo, inner_state, inner_tile, bases[0], half_inner
    )
    back_inner = swap(send_inner)
    north = after(north, send_inner)
    edge_across, head, tail = second_lat(
        lat_others,
        2 * REACH + lon_rows,
        4 * REACH + inner_rows,
        (top, bottom, inner_normed, north, south),
    )
    edge_halo = lon_halo(head, tail)
    send_edge = second(edge_across, edge_halo, edge_state, edge_tile, bases[1], edge_tiles)
    back_edge = swap(send_edge)
    edge_across = after(edge_across, send_edge, back_inner)
    keep_inner = second(edge_across, edge_halo, inner_state, inner_tile, bases[3], half_inner)
    keep_edge = second(edge_across, edge_halo, edge_state, edge_tile, bases[2], edge_tiles)
    out = jnp.zeros(fields.shape, bf16)
    edge_at = member * spare
    inner_at = other * REACH
    for piece, sample, at in (
        (keep_inner, member, inner_at),
        (keep_edge, member, edge_at),
        (back_inner, other, inner_at),
        (back_edge, other, edge_at),
    ):
        out = lax.dynamic_update_slice(out, piece[None], (sample, at, 0, 0))
    return out


def solution(mesh):
    return jax.shard_map(
        on_device,
        mesh=mesh,
        in_specs=(
            P("grp", "lat", "lon", None),
            P(),
            P(),
            P(),
            P(),
            P(),
            P(),
            P(),
            P(),
            P(("grp", "lat"), "lon"),
        ),
        out_specs=P("grp", "lat", "lon", None),
        check_vma=False,
    )
```
